256 devices in a mesh: camframe: 64 (over z_hi, y, x), row: 4 (over z_lo, core).
Axes of the slice: x: 4, y: 4, z: 8 (z_hi: 4, z_lo: 2; z = z_hi * 2 + z_lo), core: 2. Of those that a mesh axis runs over, the one named last changes fastest.
Arguments:
- tokens: bfloat16 [192, 12, 48, 1152], P('camframe', 'row'), may hold values from -40 to 40
- classes: int32 [192, 12, 48], P('camframe', 'row'), may hold values from 0 to 7
- tile_lists: int32 [192, 12, 3, 8], P('camframe', 'row'), may hold values from -1 to 11, as said below
- kv_cache: bfloat16 [192, 12, 2, 8, 2304], P('camframe', 'row'), may hold values from -200 to 200
- camera_loop: int32 [6, 2], replicated, may hold values from 0 to 5, as said below
- class_weight: bfloat16 [72, 1152], replicated, may hold values from -2 to 2
- depth_weight: bfloat16 [9, 1152], replicated, may hold values from -2 to 2
- zero_weight: bfloat16 [1152, 1152], replicated, may hold values from -0.1875 to 0.1875
- norm_gain: float32 [1152], replicated, may hold values from 0.25 to 1.75
- query_weight: bfloat16 [1152, 1152], replicated, may hold values from -0.1875 to 0.1875
- out_weight: bfloat16 [1152, 1152], replicated, may hold values from -0.1875 to 0.1875
Outputs:
- result: bfloat16 [192, 12, 48, 1152], P('camframe', 'row')
The draws below stay inside these ranges and needn't reach their ends.
Inputs may be any that keep to these rules, and one draw needn't show every extreme that they name: `tile_lists`: slot 0 of every list holds an entry below 6; the entries of one list that are not -1 are distinct. camera_loop[c, 0] and camera_loop[c, 1] are the cameras before and after camera c on one cycle through all 6 cameras.
All inputs are finite; a program needn't handle non-finite values.
Results may differ from the reference program's by a relative error of at most 0.0072.
Values may be sent and summed in bfloat16 or wider, within the bound.
No kernel may reach another device: no remote copies, remote signals or barrier semaphores. Data moves between devices by JAX's collectives and lax.ppermute only.
A program may use at most 128 MiB of HBM per device.

```python
import math
import jax
import jax.numpy as jnp
from jax import lax

D = 1152
HEADS = 16
HEAD = 72
CAMS = 6
CLASSES = 8
W = 48
TW = 8
QT = 16
K_MAX = 8
ROWS_DEV = 3
VIEWS = 192
H = 12
QPR = 3
NCAND = 12


def draw_tokens(key, part):
    key_base, key_row, key_col = jax.random.split(key, 3)
    base_vals = jnp.clip(jax.random.normal(key_base, (VIEWS, H, W, D), jnp.float32), -5.0, 5.0)
    row_scale = jnp.exp(jax.random.uniform(key_row, (VIEWS, H, W, 1), jnp.float32, math.log(0.3), math.log(3.0)))
    col_scale = jnp.exp(jax.random.uniform(key_col, (D,), jnp.float32, math.log(0.5), math.log(2.0)))
    return (base_vals * row_scale * col_scale).astype(jnp.bfloat16)


def draw_kv_cache(key, part):
    key_base = jax.random.fold_in(key, 0)
    base_vals = jnp.clip(jax.random.normal(key_base, (VIEWS, H, 2, TW, 2 * D), jnp.float32), -5.0, 5.0)
    return base_vals.astype(jnp.bfloat16)


def draw_tile_lists(key, part):
    key_first, key_order, key_keep, key_level = jax.random.split(key, 4)
    first_pick = jax.random.randint(key_first, (VIEWS, H, QPR, 1), 0, 2 * ROWS_DEV)
    ranks = jax.random.randint(key_order, (VIEWS, H, QPR, NCAND), 0, 65536) * NCAND + jnp.arange(NCAND, dtype=jnp.int32)
    ranks = jnp.where(jnp.arange(NCAND, dtype=jnp.int32) == first_pick, -1, ranks)
    order = jnp.argsort(ranks, axis=-1)[..., :K_MAX].astype(jnp.int32)
    level = jax.random.randint(key_level, (VIEWS, 1, 1, 1), 1, 4)
    keep_slot = jax.random.randint(key_keep, (VIEWS, H, QPR, K_MAX), 0, 4) < level
    keep_slot = keep_slot | (jnp.arange(K_MAX) == 0)
    return jnp.where(keep_slot, order, -1).astype(jnp.int32)


def draw_camera_loop(key, part):
    order = jax.random.permutation(key, CAMS).astype(jnp.int32)
    pairs = jnp.stack([jnp.roll(order, 1), jnp.roll(order, -1)], axis=1)
    return jnp.zeros((CAMS, 2), jnp.int32).at[order].set(pairs)


def place_ends(array, key, low, top_value):
    dims = array.shape
    spot = [jax.random.randint(jax.random.fold_in(key, axis), (), 0, dims[axis]) for axis in range(len(dims))]
    array = array.at[tuple(spot)].set(low)
    longest = dims.index(max(dims))
    spot[longest] = (spot[longest] + 1) % dims[longest]
    return array.at[tuple(spot)].set(top_value)


def centred(rng, dims, spread, limit, held_as=jnp.bfloat16):
    return jnp.clip(spread * jax.random.normal(rng, dims, jnp.float32), -limit, limit).astype(held_as)


def setup_inputs(seed: int = 0) -> dict:
    key_of = jax.random.split(jax.random.key(seed), 12)
    return {
        "tokens": draw_tokens(jax.random.fold_in(key_of[11], 71), 0),
        "classes": place_ends(jax.random.randint(key_of[1], (VIEWS, H, W), 0, CLASSES), jax.random.fold_in(key_of[1], 1), 0, CLASSES - 1).astype(jnp.int32),
        "tile_lists": draw_tile_lists(jax.random.fold_in(key_of[11], 71), 0),
        "kv_cache": draw_kv_cache(jax.random.fold_in(key_of[11], 71), 0),
        "camera_loop": draw_camera_loop(jax.random.fold_in(key_of[11], 71), 0),
        "class_weight": centred(key_of[5], (9 * CLASSES, D), 9 ** -0.5, 2.0),
        "depth_weight": centred(key_of[6], (9, D), 9 ** -0.5, 2.0),
        "zero_weight": centred(key_of[7], (D, D), D ** -0.5, 0.1875),
        "norm_gain": jnp.clip(1.0 + 0.15 * jax.random.normal(key_of[8], (D,), jnp.float32), 0.25, 1.75),
        "query_weight": centred(key_of[9], (D, D), D ** -0.5, 0.1875),
        "out_weight": centred(key_of[10], (D, D), D ** -0.5, 0.1875),
    }


def reference(tokens, classes, tile_lists, kv_cache, camera_loop, class_weight, depth_weight, zero_weight, norm_gain, query_weight, out_weight):
    score_scale = HEAD ** (-0.5)

    def one_view(view_idx):
        frame_idx = view_idx // CAMS
        camera = view_idx % CAMS
        onehot = (classes[view_idx][..., None] == jnp.arange(CLASSES, dtype=jnp.int32)).astype(jnp.float32)
        padded = jnp.pad(onehot, ((1, 1), (1, 1), (0, 0)))
        stacked = jnp.concatenate([padded[row_tap:row_tap + H, col_tap:col_tap + W] for row_tap in range(3) for col_tap in range(3)], axis=-1).astype(jnp.bfloat16)
        feature = jax.nn.silu(jnp.dot(stacked.reshape(H * W, 9 * CLASSES), class_weight, preferred_element_type=jnp.float32))
        feature = feature.astype(jnp.bfloat16).reshape(H, W, D)
        feat_pad = jnp.pad(feature.astype(jnp.float32), ((1, 1), (1, 1), (0, 0)))
        depthwise = jnp.zeros((H, W, D), jnp.float32)
        for row_tap in range(3):
            for col_tap in range(3):
                depthwise = depthwise + depth_weight[3 * row_tap + col_tap].astype(jnp.float32) * feat_pad[row_tap:row_tap + H, col_tap:col_tap + W]
        depthwise = depthwise.astype(jnp.bfloat16)
        hidden = tokens[view_idx].astype(jnp.float32).reshape(H * W, D) + jnp.dot(depthwise.reshape(H * W, D), zero_weight, preferred_element_type=jnp.float32)
        normed = (hidden * lax.rsqrt(lax.optimization_barrier(jnp.mean(hidden * hidden, axis=-1, keepdims=True)) + 1e-06) * norm_gain).astype(jnp.bfloat16)
        queries = jnp.dot(normed, query_weight, preferred_element_type=jnp.float32).astype(jnp.bfloat16)
        entry_ids = tile_lists[view_idx]
        clipped = jnp.maximum(entry_ids, 0)
        step_back = clipped // (2 * ROWS_DEV)
        side_pick = clipped // ROWS_DEV % 2
        key_row = (jnp.arange(H, dtype=jnp.int32) // ROWS_DEV * ROWS_DEV)[:, None, None] + clipped % ROWS_DEV
        live_slot = (entry_ids >= 0) & (frame_idx >= step_back)
        neighbour = jnp.where(side_pick == 0, camera_loop[camera, 0], camera_loop[camera, 1])
        source = jnp.maximum(frame_idx - step_back, 0) * CAMS + neighbour
        tile_rows = kv_cache[source, key_row, 1 - side_pick]
        key_rows = tile_rows[..., :D].astype(jnp.float32).reshape(H, QPR, K_MAX * TW, HEADS, HEAD)
        value_rows = tile_rows[..., D:].astype(jnp.float32).reshape(H, QPR, K_MAX * TW, HEADS, HEAD)
        query_heads = queries.astype(jnp.float32).reshape(H, QPR, QT, HEADS, HEAD)
        scores = jnp.einsum('yqthd,yqkhd->yqhtk', query_heads, key_rows) * score_scale
        allowed = jnp.repeat(live_slot, TW, axis=-1)[:, :, None, None, :]
        scores = jnp.where(allowed, scores, -1e+30)
        row_max = lax.optimization_barrier(jnp.max(scores, axis=-1, keepdims=True))
        exponent = jnp.exp(scores - row_max)
        weights_bf = (exponent / lax.optimization_barrier(jnp.sum(exponent, axis=-1, keepdims=True))).astype(jnp.bfloat16)
        attended = jnp.einsum('yqhtk,yqkhd->yqthd', weights_bf.astype(jnp.float32), value_rows).astype(jnp.bfloat16).reshape(H * W, D)
        result = hidden + jnp.dot(attended, out_weight, preferred_element_type=jnp.float32)
        return result.astype(jnp.bfloat16).reshape(H, W, D)
    return lax.map(one_view, jnp.arange(VIEWS, dtype=jnp.int32))
```

```python
import functools

import jax
import jax.numpy as jnp
from jax import lax
from jax.experimental import pallas as pl
from jax.experimental.pallas import tpu as pltpu
from jax.sharding import PartitionSpec as P

HEADS = 16
HEAD = 72
CLASSES = 8
QT = 16
TW = 8
LANES = 128
WIN = 256
KEYS = 128
NEG = -1e30


def dot(a, b):
    return jnp.dot(a, b, preferred_element_type=jnp.float32)


def pre_kernel(
    views,
    rows,
    cols,
    up_ref,
    own_ref,
    down_ref,
    cw_ref,
    dw_ref,
    gain_ref,
    tok_hbm,
    zw_hbm,
    qw_hbm,
    hidden_ref,
    query_ref,
    cls_buf,
    oh_buf,
    dep_buf,
    tok_buf,
    zw_buf,
    qw_buf,
    sems,
):
    copies = [
        pltpu.make_async_copy(zw_hbm, zw_buf, sems.at[0]),
        pltpu.make_async_copy(tok_hbm, tok_buf, sems.at[1]),
        pltpu.make_async_copy(qw_hbm, qw_buf, sems.at[2]),
    ]
    for copy in copies:
        copy.start()
    d_model = zw_buf.shape[0]
    ext = rows + 4
    feat_rows = rows + 2
    here = lax.axis_index("row")
    first = here == 0
    last = here == lax.axis_size("row") - 1

    cls_buf[...] = jnp.full(cls_buf.shape, -1, jnp.int32)
    for v in range(views):
        for r in range(2):
            row = up_ref[v, pl.ds(rows - 2 + r, 1), :]
            cls_buf[pl.ds(v * ext + r, 1), pl.ds(0, cols)] = jnp.where(first, -1, row)
            row = down_ref[v, pl.ds(r, 1), :]
            cls_buf[pl.ds(v * ext + 2 + rows + r, 1), pl.ds(0, cols)] = jnp.where(last, -1, row)
        for r in range(rows):
            cls_buf[pl.ds(v * ext + 2 + r, 1), pl.ds(0, cols)] = own_ref[v, pl.ds(r, 1), :]
    cells = cls_buf[...]
    shifted = (pltpu.roll(cells, 1, axis=1), cells, pltpu.roll(cells, LANES - 1, axis=1))
    kind = lax.broadcasted_iota(jnp.int32, (CLASSES, LANES), 0)
    for v in range(views):
        for y in range(feat_rows):
            taps = []
            for a in range(3):
                for b in range(3):
                    at = v * ext + y + a
                    row = jnp.broadcast_to(shifted[b][at : at + 1, :], (CLASSES, LANES))
                    taps.append(jnp.where(row == kind, 1.0, 0.0).astype(jnp.float32))
            block = jnp.concatenate(taps, axis=0).T
            oh_buf[pl.ds((v * feat_rows + y) * cols, cols), :] = block[:cols, :].astype(jnp.bfloat16)

    column = lax.broadcasted_iota(jnp.int32, (cols, LANES), 0)

    def conv(chunk, carry):
        lanes = pl.ds(pl.multiple_of(chunk * LANES, LANES), LANES)
        weight = cw_ref[:, lanes]
        taps = dw_ref[:, lanes].astype(jnp.float32)
        for v in range(views):
            onehot = oh_buf[pl.ds(v * feat_rows * cols, feat_rows * cols), :]
            raw = dot(onehot, weight)
            feat = (raw / (1.0 + jnp.exp(-raw))).astype(jnp.bfloat16).astype(jnp.float32)
            line = []
            for y in range(feat_rows):
                part = feat[y * cols : (y + 1) * cols]
                if y == 0:
                    part = jnp.where(first, 0.0, part)
                if y == feat_rows - 1:
                    part = jnp.where(last, 0.0, part)
                line.append(part)
            for y in range(rows):
                sides = []
                for b in range(3):
                    total = line[y] * taps[b : b + 1]
                    for a in (1, 2):
                        total = total + line[y + a] * taps[3 * a + b : 3 * a + b + 1]
                    sides.append(total)
                left = jnp.where(column == 0, 0.0, pltpu.roll(sides[0], 1, axis=0))
                right = jnp.where(column == cols - 1, 0.0, pltpu.roll(sides[2], cols - 1, axis=0))
                out = (sides[1] + left + right).astype(jnp.bfloat16)
                dep_buf[pl.ds((v * rows + y) * cols, cols), lanes] = out
        return carry

    lax.fori_loop(0, d_model // LANES, conv, 0)
    copies[0].wait()
    copies[1].wait()
    hidden = tok_buf[...].astype(jnp.float32) + dot(dep_buf[...], zw_buf[...])
    hidden_ref[...] = hidden
    scale = lax.rsqrt(jnp.mean(hidden * hidden, axis=-1, keepdims=True) + 1e-06)
    normed = (hidden_ref[...] * scale * gain_ref[...]).astype(jnp.bfloat16)
    copies[2].wait()
    query_ref[...] = dot(normed, qw_buf[...]).astype(jnp.bfloat16)


def relay_kernel(per_half, loop_ref, own, other, msg, sems):
    half = lax.rem(lax.axis_index("camframe"), 2)
    for i in range(per_half):
        for side in range(2):
            view = (1 - half) * per_half + i
            cam = loop_ref[view, side]
            local = lax.rem(cam, per_half)
            mine = lax.div(cam, per_half) == half
            sem = sems.at[2 * i + side]

            @pl.when(mine)
            def _():
                pltpu.make_async_copy(own.at[local, :, 1 - side], msg.at[i, side], sem).start()

            @pl.when(jnp.logical_not(mine))
            def _():
                pltpu.make_async_copy(other.at[local, :, 1 - side], msg.at[i, side], sem).start()

    for i in range(per_half):
        for side in range(2):
            pltpu.make_async_copy(own.at[0, :, 0], msg.at[i, side], sems.at[2 * i + side]).wait()


def post_kernel(
    views,
    rows,
    cols,
    loop_ref,
    list_ref,
    hidden_ref,
    query_ref,
    own,
    other,
    prev,
    ow_hbm,
    out_ref,
    kv_buf,
    ow_buf,
    live_buf,
    up_buf,
    att_buf,
    ow_sem,
    kv_sems,
):
    position = lax.axis_index("camframe")
    frame = lax.div(position, 2)
    half = lax.rem(position, 2)
    d_model = ow_buf.shape[0]
    tokens = rows * cols
    for i in range(views):
        for side in range(2):
            cam = loop_ref[half * views + i, side]
            local = lax.rem(cam, views)
            mine = lax.div(cam, views) == half
            for r in range(rows):
                spot = kv_buf.at[i, pl.ds((side * rows + r) * TW, TW)]
                sem = kv_sems.at[(2 * i + side) * rows + r]

                @pl.when(mine)
                def _():
                    pltpu.make_async_copy(own.at[local, r, 1 - side], spot, sem).start()

                @pl.when(jnp.logical_not(mine))
                def _():
                    pltpu.make_async_copy(other.at[local, r, 1 - side], spot, sem).start()

    old = []
    for i in range(views):
        old.append(
            pltpu.make_async_copy(
                prev.at[i],
                kv_buf.at[i, pl.ds(2 * rows * TW, 2 * rows * TW)],
                kv_sems.at[2 * views * rows + i],
            )
        )
        old[-1].start()
    weight = pltpu.make_async_copy(ow_hbm, ow_buf, ow_sem)
    weight.start()
    pad = KEYS - 4 * rows * TW
    for i in range(views):
        kv_buf[i, pl.ds(KEYS - pad, pad), :] = jnp.zeros((pad, 2 * d_model), jnp.bfloat16)

    entry = lax.broadcasted_iota(jnp.int32, (cols // QT, KEYS), 1) // TW
    known = jnp.logical_or(entry < 2 * rows, frame > 0)
    for v in range(views):
        for r in range(rows):
            lists = list_ref[v, r]
            hit = jnp.zeros((cols // QT, KEYS), jnp.int32)
            for k in range(lists.shape[1]):
                hit = jnp.where(lists[:, k : k + 1] == entry, 1, hit)
            hit = jnp.where(known, hit, 0)
            for q in range(cols // QT):
                live_buf[v, pl.ds(r * cols + q * QT, QT), :] = jnp.broadcast_to(
                    hit[q : q + 1, :], (QT, KEYS)
                )

    for i in range(views):
        for side in range(2):
            for r in range(rows):
                spot = kv_buf.at[i, pl.ds((side * rows + r) * TW, TW)]
                sem = kv_sems.at[(2 * i + side) * rows + r]
                pltpu.make_async_copy(own.at[0, 0, 0], spot, sem).wait()
        old[i].wait()

    up_buf[...] = jnp.zeros_like(up_buf)
    score_scale = HEAD ** (-0.5)
    lane = lax.broadcasted_iota(jnp.int32, (KEYS, WIN), 1)

    def attend(pair, carry):
        base = pl.multiple_of(pair * LANES, LANES)
        start = pair * (2 * HEAD - LANES)
        heads = []
        for h in range(2):
            low = start + h * HEAD
            heads.append(jnp.logical_and(lane >= low, lane < low + HEAD))
        for v in range(views):
            query = query_ref[pl.ds(v * tokens, tokens), pl.ds(base, WIN)]
            key = kv_buf[v, :, pl.ds(base, WIN)]
            value = kv_buf[v, :, pl.ds(pl.multiple_of(base + d_model, LANES), WIN)]
            zero = jnp.zeros_like(key)
            keys = jnp.concatenate([jnp.where(m, key, zero) for m in heads], axis=0)
            values = jnp.concatenate([jnp.where(m, value, zero) for m in heads], axis=0)
            scores = lax.dot_general(
                query, keys, (((1,), (1,)), ((), ())), preferred_element_type=jnp.float32
            )
            live = live_buf[v] > 0
            probs = []
            for h in range(2):
                s = jnp.where(live, scores[:, h * KEYS : (h + 1) * KEYS] * score_scale, NEG)
                e = jnp.exp(s - jnp.max(s, axis=-1, keepdims=True))
                probs.append((e / jnp.sum(e, axis=-1, keepdims=True)).astype(jnp.bfloat16))
            got = dot(jnp.concatenate(probs, axis=1), values)
            att_buf[pl.ds(v * tokens, tokens), pl.ds(base, LANES)] = (
                got[:, :LANES] + up_buf[v]
            ).astype(jnp.bfloat16)
            up_buf[v] = got[:, LANES:]
        return carry

    lax.fori_loop(0, HEADS // 2, attend, 0)
    for v in range(views):
        att_buf[pl.ds(v * tokens, tokens), pl.ds(d_model - LANES, LANES)] = up_buf[v].astype(
            jnp.bfloat16
        )
    weight.wait()
    out_ref[...] = (hidden_ref[...] + dot(att_buf[...], ow_buf[...])).astype(jnp.bfloat16)


def body(
    tokens,
    classes,
    tile_lists,
    kv_cache,
    camera_loop,
    class_weight,
    depth_weight,
    zero_weight,
    norm_gain,
    query_weight,
    out_weight,
):
    views, rows, cols, d_model = tokens.shape
    count = views * rows * cols
    vmem = pl.BlockSpec(memory_space=pltpu.VMEM)
    smem = pl.BlockSpec(memory_space=pltpu.SMEM)
    hbm = pl.BlockSpec(memory_space=pl.ANY)
    params = pltpu.CompilerParams(vmem_limit_bytes=56 * 1024 * 1024)

    frames2 = lax.axis_size("camframe")
    ends = lax.axis_size("row") - 1
    other = lax.ppermute(kv_cache, "camframe", [(i, i ^ 1) for i in range(frames2)])
    up = lax.ppermute(classes, "row", [(i, i + 1) for i in range(ends)])
    down = lax.ppermute(classes, "row", [(i + 1, i) for i in range(ends)])

    hidden, queries = pl.pallas_call(
        functools.partial(pre_kernel, views, rows, cols),
        out_shape=(
            jax.ShapeDtypeStruct((count, d_model), jnp.float32),
            jax.ShapeDtypeStruct((count, d_model), jnp.bfloat16),
        ),
        in_specs=[vmem] * 6 + [hbm] * 3,
        out_specs=(vmem, vmem),
        scratch_shapes=[
            pltpu.VMEM((-(-views * (rows + 4) // 8) * 8, LANES), jnp.int32),
            pltpu.VMEM((views * (rows + 2) * cols, 9 * CLASSES), jnp.bfloat16),
            pltpu.VMEM((count, d_model), jnp.bfloat16),
            pltpu.VMEM((count, d_model), jnp.bfloat16),
            pltpu.VMEM((d_model, d_model), jnp.bfloat16),
            pltpu.VMEM((d_model, d_model), jnp.bfloat16),
            pltpu.SemaphoreType.DMA((3,)),
        ],
        compiler_params=params,
        name="pre",
    )(
        up,
        classes,
        down,
        class_weight,
        depth_weight,
        norm_gain.reshape(1, d_model),
        tokens.reshape(count, d_model),
        zero_weight,
        query_weight,
    )

    edge = kv_cache.shape[3]
    msg = pl.pallas_call(
        functools.partial(relay_kernel, views),
        out_shape=jax.ShapeDtypeStruct((views, 2, rows, edge, 2 * d_model), jnp.bfloat16),
        in_specs=[smem, hbm, hbm],
        out_specs=hbm,
        scratch_shapes=[pltpu.SemaphoreType.DMA((2 * views,))],
        compiler_params=params,
        name="relay",
    )(camera_loop, kv_cache, other)
    route = [(i, (i // 2 + 1) * 2 + 1 - i % 2) for i in range(frames2 - 2)]
    prev = lax.ppermute(msg, "camframe", route)

    result = pl.pallas_call(
        functools.partial(post_kernel, views, rows, cols),
        out_shape=jax.ShapeDtypeStruct((count, d_model), jnp.bfloat16),
        in_specs=[smem] + [vmem] * 3 + [hbm] * 4,
        out_specs=vmem,
        scratch_shapes=[
            pltpu.VMEM((views, KEYS, 2 * d_model), jnp.bfloat16),
            pltpu.VMEM((d_model, d_model), jnp.bfloat16),
            pltpu.VMEM((views, rows * cols, KEYS), jnp.int32),
            pltpu.VMEM((views, rows * cols, LANES), jnp.float32),
            pltpu.VMEM((count, d_model), jnp.bfloat16),
            pltpu.SemaphoreType.DMA,
            pltpu.SemaphoreType.DMA((2 * views * rows + views,)),
        ],
        compiler_params=params,
        name="post",
    )(
        camera_loop,
        tile_lists,
        hidden,
        queries,
        kv_cache,
        other,
        prev.reshape(views, 2 * rows * edge, 2 * d_model),
        out_weight,
    )
    return result.reshape(views, rows, cols, d_model)


def solution(mesh):
    return jax.shard_map(
        body,
        mesh=mesh,
        in_specs=(
            P("camframe", "row", None, None),
            P("camframe", "row", None),
            P("camframe", "row", None, None),
            P("camframe", "row", None, None, None),
            P(),
            P(),
            P(),
            P(),
            P(),
            P(),
            P(),
        ),
        out_specs=P("camframe", "row", None, None),
        check_vma=False,
    )
```
